32 devices in a mesh: dp: 4 (over z), row: 2 (over y), col: 4 (over x, core).
Axes of the slice: x: 2, y: 2, z: 4, core: 2. Of those that a mesh axis runs over, the one named last changes fastest.
Arguments:
- residual: bfloat16 [4096, 2048], P('dp', ('row', 'col')), may hold values from -6 to 6
- doc_ids: int32 [4096], P(('dp', 'row')), may hold values from 0 to 15, never falling along the last dimension, each value on 1 to 500 neighbouring positions
- attn_gain: float32 [2048], P(('row', 'col')), may hold values from 0.5 to 1.5
- w_query: bfloat16 [2048, 2048], P('row', 'col'), may hold values from -0.125 to 0.125
- w_key: bfloat16 [2048, 2048], P('row', 'col'), may hold values from -0.125 to 0.125
- w_value: bfloat16 [2048, 4096], P('row', 'col'), may hold values from -0.125 to 0.125
- w_gate: bfloat16 [2048, 4096], P('row', 'col'), may hold values from -0.125 to 0.125
- group_gain: float32 [4096], P('col'), may hold values from 0.5 to 1.5
- w_out: bfloat16 [4096, 2048], P('col', 'row'), may hold values from -0.09375 to 0.09375
- mlp_gain: float32 [2048], P(('row', 'col')), may hold values from 0.5 to 1.5
- w_act: bfloat16 [2048, 4096], P('row', 'col'), may hold values from -0.125 to 0.125
- w_lin: bfloat16 [2048, 4096], P('row', 'col'), may hold values from -0.125 to 0.125
- w_down: bfloat16 [4096, 2048], P('col', 'row'), may hold values from -0.09375 to 0.09375
- cotangent: bfloat16 [4096, 2048], P('dp', ('row', 'col')), may hold values from -6 to 6
Outputs:
- output: bfloat16 [4096, 2048], P('dp', ('row', 'col'))
- grad_input: float32 [4096, 2048], P('dp', ('row', 'col'))
- grad_query: float32 [2048, 2048], P('row', 'col')
- grad_key: float32 [2048, 2048], P('row', 'col')
- grad_value: float32 [2048, 4096], P('row', 'col')
- grad_gate: float32 [2048, 4096], P('row', 'col')
- grad_out: float32 [4096, 2048], P('col', 'row')
- grad_act: float32 [2048, 4096], P('row', 'col')
- grad_lin: float32 [2048, 4096], P('row', 'col')
- grad_down: float32 [4096, 2048], P('col', 'row')
- grad_first: float32 [2048], P(('row', 'col'))
- grad_second: float32 [2048], P(('row', 'col'))
- grad_group: float32 [4096], P('col')
The draws below stay inside these ranges and needn't reach their ends.
Inputs may be any that keep to these rules, and one draw needn't show every extreme that they name: `doc_ids`: document numbers never fall along the tokens; a document has at most 500 tokens, and some document has exactly that many; documents may run on across the bounds of sequences.
All inputs are finite; a program needn't handle non-finite values.
Results may differ from the reference program's by a relative error of at most 0.015.
Values may be sent and summed in bfloat16 or wider, within the bound.
No kernel may reach another device: no remote copies, remote signals or barrier semaphores. Data moves between devices by JAX's collectives and lax.ppermute only.
A program may use at most 192 MiB of HBM per device.

```python
import math
import jax
import jax.numpy as jnp
import numpy as np
from jax import lax

D = 2048
H = 8
DK = 256
DV = 512
FF = 4096
LEN = 512
BLOCK = 512
HK = 2048
VALUE_WIDTH_ALL = 4096
TOKENS = 4096


def block_levels(rng, extent, shards, least, top_value):
    def one(axis_at, blocks):
        steps = jax.random.uniform(jax.random.fold_in(jax.random.fold_in(rng, 6), axis_at), (blocks,), jnp.float32, least / len(shards), top_value / len(shards))
        return jnp.repeat(jnp.exp(steps), extent[axis_at] // blocks).reshape((-1,) + (1,) * (len(extent) - axis_at - 1))

    factor_of = one(*shards[0])
    for cut in shards[1:]:
        factor_of = factor_of * one(*cut)
    return factor_of


def length_profile(count, total, limit, skew):
    portions = [(1 << 20) // math.isqrt(grade ** skew) + 1 for grade in range(2, count + 1)]
    rest, holding = total - limit - (count - 1), [1] * (count - 1)
    while rest > 0:
        free = [i for i in range(count - 1) if holding[i] < limit]
        pool, left = sum([portions[i] for i in free]), rest
        for i in free:
            addition = min(limit - holding[i], max(1, left * portions[i] // pool), rest)
            holding[i] = holding[i] + addition
            rest = rest - addition
    return np.array([limit] + holding)


def uneven(own_key, number_of, total, most, skew):
    if number_of == 2:
        one = jax.random.randint(own_key, (), max(1, total - most), min(most, total - 1) + 1)
        return jnp.stack([one, total - one])
    lengths = jnp.asarray(length_profile(number_of, total, most, skew), jnp.int32)
    pairs = (number_of - 1) // 2
    donor, taker = lengths[1:1 + 2 * pairs:2], lengths[2:2 + 2 * pairs:2]
    room = jnp.minimum(donor - 1, most - taker)
    shifted = jax.random.randint(jax.random.fold_in(own_key, 1), (pairs,), 0, 1 << 20) % (room + 1)
    lengths = lengths.at[1:1 + 2 * pairs:2].set(donor - shifted).at[2:2 + 2 * pairs:2].set(taker + shifted)
    return lengths[jax.random.permutation(jax.random.fold_in(own_key, 2), number_of)]


def bell_draw(stream_key, dims, width, reach, shards=(), held_as=jnp.bfloat16):
    array = width * jax.random.normal(stream_key, dims, jnp.float32)
    if shards:
        array = array * block_levels(stream_key, dims, shards, -0.22, 0.18)
    return jnp.clip(array, -reach, reach).astype(held_as)


def setup_inputs(seed: int = 0) -> dict:
    key_of = jax.random.split(jax.random.key(seed), 15)
    return {
        "residual": bell_draw(key_of[0], (TOKENS, D), 1.0, 6.0, ((0, 4), (1, 8))),
        "doc_ids": jnp.searchsorted(jnp.cumsum(uneven(key_of[1], TOKENS * 2 // LEN, TOKENS, LEN * 125 // 128, 0)), jnp.arange(TOKENS), side="right").astype(jnp.int32),
        "attn_gain": jnp.clip(1.0 + 0.1 * jax.random.normal(key_of[2], (D,), jnp.float32), 0.5, 1.5),
        "w_query": bell_draw(key_of[3], (D, HK), D ** -0.5, 0.125, ((0, 2), (1, 4))),
        "w_key": bell_draw(key_of[4], (D, HK), D ** -0.5, 0.125, ((0, 2), (1, 4))),
        "w_value": bell_draw(key_of[5], (D, VALUE_WIDTH_ALL), D ** -0.5, 0.125, ((0, 2), (1, 4))),
        "w_gate": bell_draw(key_of[6], (D, VALUE_WIDTH_ALL), D ** -0.5, 0.125, ((0, 2), (1, 4))),
        "group_gain": jnp.clip(1.0 + 0.1 * jax.random.normal(key_of[7], (VALUE_WIDTH_ALL,), jnp.float32), 0.5, 1.5),
        "w_out": bell_draw(key_of[8], (VALUE_WIDTH_ALL, D), VALUE_WIDTH_ALL ** -0.5, 0.09375, ((0, 4), (1, 2))),
        "mlp_gain": jnp.clip(1.0 + 0.1 * jax.random.normal(key_of[9], (D,), jnp.float32), 0.5, 1.5),
        "w_act": bell_draw(key_of[10], (D, FF), D ** -0.5, 0.125, ((0, 2), (1, 4))),
        "w_lin": bell_draw(key_of[11], (D, FF), D ** -0.5, 0.125, ((0, 2), (1, 4))),
        "w_down": bell_draw(key_of[12], (FF, D), FF ** -0.5, 0.09375, ((0, 4), (1, 2))),
        "cotangent": bell_draw(key_of[13], (TOKENS, D), 1.0, 6.0, ((0, 4), (1, 8))),
    }


EPSILON = 1e-05
GROUP_EPSILON = 1.0
ROOT_TWO = math.sqrt(2.0)
ROOT_TWO_PI = math.sqrt(2.0 * math.pi)

def wide_product(left_rows, right_rows):
    return jnp.dot(left_rows, right_rows, preferred_element_type=jnp.float32)

def decay_logs(first_head, head_count):
    numbers = (first_head + jnp.arange(head_count, dtype=jnp.int32)).astype(jnp.float32)
    return jnp.log(1.0 - jnp.exp2(-5.0 - numbers))

def decay_mask(seq_ids, log_decay, first_row):
    query_pos = first_row + jnp.arange(BLOCK, dtype=jnp.int32)
    key_pos = jnp.arange(seq_ids.shape[0], dtype=jnp.int32)
    query_ids = lax.dynamic_slice_in_dim(seq_ids, first_row, BLOCK, 0)
    distance = query_pos[:, None] - key_pos[None, :]
    allowed = (distance >= 0) & (query_ids[:, None] == seq_ids[None, :])
    elapsed = jnp.maximum(distance, 0).astype(jnp.float32)
    decays = jnp.exp(log_decay[:, None, None] * elapsed[None])
    return jnp.where(allowed[None], decays, 0.0)

def retention_forward(query_heads, key_heads, value_heads, seq_ids, log_decay):
    score_scale = 1.0 / math.sqrt(DK)
    key_wide = key_heads.astype(jnp.float32)
    value_wide = value_heads.astype(jnp.float32)
    starts = jnp.arange(LEN // BLOCK, dtype=jnp.int32) * BLOCK

    def one_block(first_row):
        rows_query = lax.dynamic_slice_in_dim(query_heads, first_row, BLOCK, 0).astype(jnp.float32)
        scores = jnp.einsum('chd,lhd->hcl', rows_query, key_wide) * score_scale
        rounded = lax.optimization_barrier((scores * decay_mask(seq_ids, log_decay, first_row)).astype(jnp.bfloat16))
        return jnp.einsum('hcl,lhd->chd', rounded.astype(jnp.float32), value_wide)
    blocks = lax.map(one_block, starts)
    return blocks.reshape(LEN, query_heads.shape[1], value_heads.shape[2])

def retention_backward(query_heads, key_heads, value_heads, grad_heads, seq_ids, log_decay):
    score_scale = 1.0 / math.sqrt(DK)
    query_wide = query_heads.astype(jnp.float32)
    key_wide = key_heads.astype(jnp.float32)
    value_wide = value_heads.astype(jnp.float32)
    grad_wide = grad_heads.astype(jnp.float32)
    starts = jnp.arange(LEN // BLOCK, dtype=jnp.int32) * BLOCK

    def one_block(carry, first_row):
        key_acc, value_acc = carry
        rows_query = lax.dynamic_slice_in_dim(query_wide, first_row, BLOCK, 0)
        rows_grad = lax.dynamic_slice_in_dim(grad_wide, first_row, BLOCK, 0)
        mask = decay_mask(seq_ids, log_decay, first_row)
        scores = jnp.einsum('chd,lhd->hcl', rows_query, key_wide) * score_scale
        rounded = lax.optimization_barrier((scores * mask).astype(jnp.bfloat16)).astype(jnp.float32)
        d_weights = jnp.einsum('chd,lhd->hcl', rows_grad, value_wide)
        value_acc = value_acc + jnp.einsum('hcl,chd->lhd', rounded, rows_grad)
        d_scores = lax.optimization_barrier((d_weights * mask * score_scale).astype(jnp.bfloat16)).astype(jnp.float32)
        query_out = jnp.einsum('hcl,lhd->chd', d_scores, key_wide)
        key_acc = key_acc + jnp.einsum('hcl,chd->lhd', d_scores, rows_query)
        return ((key_acc, value_acc), query_out)
    start_carry = (jnp.zeros(key_heads.shape, jnp.float32), jnp.zeros(value_heads.shape, jnp.float32))
    (key_acc, value_acc), query_blocks = lax.scan(one_block, start_carry, starts)
    return (query_blocks.reshape(query_heads.shape), key_acc, value_acc)

def layer_norm(stream, gain):
    center = lax.optimization_barrier(jnp.mean(stream, axis=1, keepdims=True))
    variance = lax.optimization_barrier(jnp.mean(stream * stream, axis=1, keepdims=True)) - center * center
    inv_std = lax.rsqrt(variance + EPSILON)
    normed = (stream - center) * inv_std
    return (normed, inv_std, (normed * gain).astype(jnp.bfloat16))

def norm_backward(grad_norm, normed, inv_std, gain):
    scaled = grad_norm * gain
    mean_one = lax.optimization_barrier(jnp.mean(scaled, axis=1, keepdims=True))
    mean_two = lax.optimization_barrier(jnp.mean(scaled * normed, axis=1, keepdims=True))
    return inv_std * (scaled - mean_one - normed * mean_two)

def group_norm(retained):
    center = lax.optimization_barrier(jnp.mean(retained, axis=2, keepdims=True))
    variance = lax.optimization_barrier(jnp.mean(retained * retained, axis=2, keepdims=True)) - center * center
    inv_std = lax.rsqrt(variance + GROUP_EPSILON)
    return ((retained - center) * inv_std, inv_std)

def gelu_parts(act_pre):
    normal_cdf = 0.5 * (1.0 + jax.scipy.special.erf(act_pre / ROOT_TWO))
    slope = normal_cdf + act_pre * jnp.exp(-0.5 * act_pre * act_pre) / ROOT_TWO_PI
    return (act_pre * normal_cdf, slope)

def reference(residual, doc_ids, attn_gain, w_query, w_key, w_value, w_gate, group_gain, w_out, mlp_gain, w_act, w_lin, w_down, cotangent):
    seq_total = TOKENS // LEN
    log_decay = decay_logs(0, H)
    gain_heads = group_gain.reshape(H, DV)

    def one_sequence(total_sums, members):
        tokens_in, seq_ids, sequence_gradient = members
        stream = tokens_in.astype(jnp.float32)
        first_normed, inv_one, first_input = layer_norm(stream, attn_gain)
        query_heads = wide_product(first_input, w_query).astype(jnp.bfloat16).reshape(LEN, H, DK)
        key_heads = wide_product(first_input, w_key).astype(jnp.bfloat16).reshape(LEN, H, DK)
        value_heads = wide_product(first_input, w_value).astype(jnp.bfloat16).reshape(LEN, H, DV)
        gate_heads = wide_product(first_input, w_gate).reshape(LEN, H, DV)
        retained = retention_forward(query_heads, key_heads, value_heads, seq_ids, log_decay)
        group_normed_output, inv_group = group_norm(retained)
        sigmoid_gate = jax.nn.sigmoid(gate_heads)
        swish_output = gate_heads * sigmoid_gate
        gate_applied = (swish_output * group_normed_output * gain_heads).astype(jnp.bfloat16).reshape(LEN, VALUE_WIDTH_ALL)
        middle = stream + wide_product(gate_applied, w_out)
        second_normed, inv_two, second_input = layer_norm(middle, mlp_gain)
        act_pre = wide_product(second_input, w_act)
        lin_pre = wide_product(second_input, w_lin)
        gelu_value, gelu_slope = gelu_parts(act_pre)
        hidden_state = (gelu_value * lin_pre).astype(jnp.bfloat16)
        output = (middle + wide_product(hidden_state, w_down)).astype(jnp.bfloat16)
        d_hidden = wide_product(sequence_gradient, w_down.T)
        activation_gradient = (d_hidden * lin_pre * gelu_slope).astype(jnp.bfloat16)
        linear_gradient = (d_hidden * gelu_value).astype(jnp.bfloat16)
        second_norm_gradient = wide_product(activation_gradient, w_act.T) + wide_product(linear_gradient, w_lin.T)
        d_middle = sequence_gradient.astype(jnp.float32) + norm_backward(second_norm_gradient, second_normed, inv_two, mlp_gain)
        middle_gradient = d_middle.astype(jnp.bfloat16)
        head_gradients = wide_product(middle_gradient, w_out.T).reshape(LEN, H, DV)
        swish_slope = sigmoid_gate * (1.0 + gate_heads * (1.0 - sigmoid_gate))
        gate_gradient = (head_gradients * group_normed_output * gain_heads * swish_slope).astype(jnp.bfloat16).reshape(LEN, VALUE_WIDTH_ALL)
        d_group = head_gradients * swish_output * gain_heads
        d_retained = inv_group * (d_group - lax.optimization_barrier(jnp.mean(d_group, axis=2, keepdims=True)) - group_normed_output * lax.optimization_barrier(jnp.mean(d_group * group_normed_output, axis=2, keepdims=True)))
        d_retained = d_retained.astype(jnp.bfloat16)
        d_query, d_key, d_value = retention_backward(query_heads, key_heads, value_heads, d_retained, seq_ids, log_decay)
        query_gradient = d_query.astype(jnp.bfloat16).reshape(LEN, HK)
        key_gradient = d_key.astype(jnp.bfloat16).reshape(LEN, HK)
        value_gradient = d_value.astype(jnp.bfloat16).reshape(LEN, VALUE_WIDTH_ALL)
        first_norm_gradient = wide_product(query_gradient, w_query.T) + wide_product(key_gradient, w_key.T) + wide_product(value_gradient, w_value.T) + wide_product(gate_gradient, w_gate.T)
        grad_seq_in = d_middle + norm_backward(first_norm_gradient, first_normed, inv_one, attn_gain)
        partial_terms = (wide_product(first_input.T, query_gradient), wide_product(first_input.T, key_gradient), wide_product(first_input.T, value_gradient), wide_product(first_input.T, gate_gradient), wide_product(gate_applied.T, middle_gradient), wide_product(second_input.T, activation_gradient), wide_product(second_input.T, linear_gradient), wide_product(hidden_state.T, sequence_gradient), lax.optimization_barrier(jnp.sum(first_norm_gradient * first_normed, axis=0)), lax.optimization_barrier(jnp.sum(second_norm_gradient * second_normed, axis=0)), lax.optimization_barrier(jnp.sum(head_gradients * swish_output * group_normed_output, axis=0)).reshape(VALUE_WIDTH_ALL))
        total_sums = tuple((running_total + partial_term for running_total, partial_term in zip(total_sums, partial_terms)))
        return (total_sums, (output, grad_seq_in))
    zero_grads = (jnp.zeros((D, HK), jnp.float32), jnp.zeros((D, HK), jnp.float32), jnp.zeros((D, VALUE_WIDTH_ALL), jnp.float32), jnp.zeros((D, VALUE_WIDTH_ALL), jnp.float32), jnp.zeros((VALUE_WIDTH_ALL, D), jnp.float32), jnp.zeros((D, FF), jnp.float32), jnp.zeros((D, FF), jnp.float32), jnp.zeros((FF, D), jnp.float32), jnp.zeros((D,), jnp.float32), jnp.zeros((D,), jnp.float32), jnp.zeros((VALUE_WIDTH_ALL,), jnp.float32))
    members = (residual.reshape(seq_total, LEN, D), doc_ids.reshape(seq_total, LEN), cotangent.reshape(seq_total, LEN, D))
    total_sums, (outputs, grads_in) = lax.scan(one_sequence, zero_grads, members)
    return (outputs.reshape(TOKENS, D), grads_in.reshape(TOKENS, D), total_sums[0], total_sums[1], total_sums[2], total_sums[3], total_sums[4], total_sums[5], total_sums[6], total_sums[7], total_sums[8], total_sums[9], total_sums[10])
```

```python
import math

import jax
import jax.numpy as jnp
from jax import lax
from jax.sharding import PartitionSpec as P

D = 2048
DK = 256
DV = 512
LEN = 512

EPSILON = 1e-05
GROUP_EPSILON = 1.0
ROOT_TWO = math.sqrt(2.0)
ROOT_TWO_PI = math.sqrt(2.0 * math.pi)
F32 = jnp.float32
BF16 = jnp.bfloat16


def mm(left, right, dims):
    return lax.dot_general(left, right, ((dims[:1], dims[1:]), ((), ())), preferred_element_type=F32)


def ordered(first, *rest):
    return lax.optimization_barrier((first, *rest))


class Grid:
    def __init__(self):
        self.dp = lax.axis_size("dp")
        self.cols = lax.axis_size("col")
        self.row = lax.axis_index("row")
        self.col = lax.axis_index("col")
        self.z = lax.axis_index("dp")
        self.core = self.col % 2
        self.x = self.col // 2
        self.half = jnp.bitwise_xor(self.core, self.row)
        self.x_bits = [1 << b for b in range(1, self.cols.bit_length() - 1)]

    def swap_row(self, a):
        return lax.ppermute(a, "row", [(0, 1), (1, 0)])

    def swap_col(self, a, bit):
        return lax.ppermute(a, "col", [(i, i ^ bit) for i in range(self.cols)])

    def swap_core(self, a):
        return self.swap_col(a, 1)

    def pick(self, flag, a, b):
        return jnp.where(flag == 0, a, b)

    def halves(self, first, second, index):
        return self.pick(index, first, second), self.pick(index, second, first)

    def gather_cols(self, a):
        for bit in self.x_bits:
            got = self.swap_col(a, bit)
            flag = jnp.bitwise_and(self.col, bit)
            a = self.pick(flag, jnp.concatenate([a, got], 1), jnp.concatenate([got, a], 1))
        got = self.swap_core(a)
        low, high = self.pick(self.core, a, got), self.pick(self.core, got, a)
        width = a.shape[1] // (self.cols // 2)
        parts = []
        for i in range(self.cols // 2):
            cut = slice(i * width, (i + 1) * width)
            parts += [low[:, cut], high[:, cut]]
        return jnp.concatenate(parts, 1)

    def sum_chips(self, a):
        for bit in self.x_bits:
            a = a + self.swap_col(a.astype(BF16), bit).astype(F32)
        return a

    def x_block(self, a, x):
        width = a.shape[1] // (self.cols // 2)
        return lax.dynamic_slice_in_dim(a, x * width, width, 1)

    def scatter_chips(self, a):
        bits = self.x_bits[::-1]
        for bit in bits:
            width = a.shape[1] // 2
            low, high = a[:, :width], a[:, width:]
            flag = jnp.bitwise_and(self.col, bit)
            keep, send = self.pick(flag, low, high), self.pick(flag, high, low)
            a = keep + self.swap_col(send.astype(BF16), bit).astype(F32)
        return a

    def to_blocks(self, a):
        width = a.shape[1] // 2
        low, high = a[:, :width], a[:, width:]
        keep, send = self.pick(self.core, low, high), self.pick(self.core, high, low)
        got = self.swap_core(send)
        first, second = self.halves(keep, got, self.half)
        return jnp.concatenate([first, second], 0)

    def sum_tokens_over_row(self, a):
        return a + self.swap_row(a)

    def reduce_dp(self, grad):
        if self.dp != 4:
            return lax.psum(grad.astype(F32), "dp")
        middle = (self.z == 1) | (self.z == 2)
        pair = grad.astype(F32) + lax.ppermute(grad, "dp", [(0, 1), (3, 2)]).astype(F32)
        pair = pair.astype(BF16)
        total = pair.astype(F32) + lax.ppermute(pair, "dp", [(1, 2), (2, 1)]).astype(F32)
        total = total.astype(BF16)
        ends = lax.ppermute(total, "dp", [(1, 0), (2, 3)])
        return jnp.where(middle, total, ends).astype(F32)


def decay_logs(first_head, head_count):
    numbers = (first_head + jnp.arange(head_count, dtype=jnp.int32)).astype(F32)
    return jnp.log(1.0 - jnp.exp2(-5.0 - numbers))


def decay_mask(seq_ids, log_decay):
    position = jnp.arange(LEN, dtype=jnp.int32)
    distance = position[:, None] - position[None, :]
    allowed = (distance >= 0)[None] & (seq_ids[:, :, None] == seq_ids[:, None, :])
    elapsed = jnp.maximum(distance, 0).astype(F32)
    decays = jnp.exp(log_decay[:, None, None] * elapsed[None])
    return jnp.where(allowed[:, None], decays[None], 0.0)


def gelu_parts(act_pre):
    normal_cdf = 0.5 * (1.0 + jax.scipy.special.erf(act_pre / ROOT_TWO))
    slope = normal_cdf + act_pre * jnp.exp(-0.5 * act_pre * act_pre) / ROOT_TWO_PI
    return (act_pre * normal_cdf, slope)


def body(
    residual,
    doc_ids,
    attn_gain,
    w_query,
    w_key,
    w_value,
    w_gate,
    group_gain,
    w_out,
    mlp_gain,
    w_act,
    w_lin,
    w_down,
    cotangent,
):
    g = Grid()
    heads = w_query.shape[1] // DK
    own = doc_ids.shape[0]
    seqs = own // LEN
    log_decay = decay_logs(g.col * heads, heads)
    gain_heads = group_gain.reshape(heads, DV)

    def roll(a):
        return g.pick(g.row, a, jnp.concatenate([a[own:], a[:own]], 0))

    res_block, cot_block = roll(residual), roll(cotangent)
    wide = res_block.astype(F32)
    stats = jnp.stack([jnp.sum(wide, 1), jnp.sum(wide * wide, 1)])
    res = g.gather_cols(res_block)
    stats = stats + g.swap_core(stats)
    for bit in g.x_bits:
        stats = stats + g.swap_col(stats, bit)
    got = g.swap_row(stats)
    stats = stats + jnp.concatenate([got[:, own:], got[:, :own]], 1)
    gains = g.gather_cols(jnp.stack([attn_gain, mlp_gain]))
    gain_one, gain_two = gains[0], gains[1]
    center = stats[0] / D
    rstd_one = lax.rsqrt(stats[1] / D - center * center + EPSILON)
    normed_one = (res.astype(F32) - center[:, None]) * rstd_one[:, None]
    h1 = (normed_one * gain_one).astype(BF16)

    def spread(rows, weight, dim):
        sent = g.swap_row(mm(rows[own:], weight, (1, dim)).astype(BF16))
        return mm(rows[:own], weight, (1, dim)) + sent.astype(F32)

    q = spread(h1, w_query, 0).astype(BF16).reshape(seqs, LEN, heads, DK)
    k = spread(h1, w_key, 0).astype(BF16).reshape(seqs, LEN, heads, DK)
    v = spread(h1, w_value, 0).astype(BF16).reshape(seqs, LEN, heads, DV)
    gate = spread(h1, w_gate, 0).reshape(own, heads, DV)

    cot = g.gather_cols(cot_block)
    d_hidden = spread(cot, w_down, 1)

    mask = decay_mask(doc_ids.reshape(seqs, LEN), log_decay) * (1.0 / math.sqrt(DK))
    scores = jnp.einsum("schd,slhd->shcl", q, k, preferred_element_type=F32)
    weights = (scores * mask).astype(BF16)
    retained = jnp.einsum("shcl,slhd->schd", weights, v, preferred_element_type=F32)
    retained = retained.reshape(own, heads, DV)
    center_o = jnp.mean(retained, axis=2, keepdims=True)
    var_o = jnp.mean(retained * retained, axis=2, keepdims=True) - center_o * center_o
    rstd_o = lax.rsqrt(var_o + GROUP_EPSILON)
    on = (retained - center_o) * rstd_o
    sig = jax.nn.sigmoid(gate)
    swish = gate * sig
    z = (swish * on * gain_heads).astype(BF16).reshape(own, heads * DV)
    z_other = g.swap_row(z)

    def sum_cols(product):
        sent = g.swap_core(product(1).astype(BF16))
        return product(0) + sent.astype(F32)

    z_keep, z_send = g.halves(z, z_other, g.half)
    attn = g.sum_chips(sum_cols(lambda i: mm((z_keep, z_send)[i], w_out, (1, 0))))
    res_half = g.pick(g.half, res[:own], res[own:])
    cot_half = g.pick(g.half, cot[:own], cot[own:])
    middle = res_half.astype(F32) + attn
    stats_two = jnp.stack([jnp.sum(middle, 1), jnp.sum(middle * middle, 1)])
    stats_two = stats_two + g.swap_row(stats_two)
    center = stats_two[0] / D
    rstd_two = lax.rsqrt(stats_two[1] / D - center * center + EPSILON)[:, None]
    normed_two = (middle - center[:, None]) * rstd_two
    h2_half = (normed_two * gain_two).astype(BF16)
    h2 = jnp.concatenate(g.halves(h2_half, g.swap_core(h2_half), g.half), 0)

    act = spread(h2, w_act, 0)
    lin = spread(h2, w_lin, 0)
    gelu, slope = gelu_parts(act)
    d_act = (d_hidden * lin * slope).astype(BF16)
    d_lin = (d_hidden * gelu).astype(BF16)
    u = (gelu * lin).astype(BF16)
    d_act_other = g.swap_row(d_act)
    d_lin_other = g.swap_row(d_lin)
    u_other = g.swap_row(u)

    d_act_keep, d_act_send = g.halves(d_act, d_act_other, g.half)
    d_lin_keep, d_lin_send = g.halves(d_lin, d_lin_other, g.half)

    def d_second(i):
        return mm((d_act_keep, d_act_send)[i], w_act, (1, 1)) + mm(
            (d_lin_keep, d_lin_send)[i], w_lin, (1, 1)
        )

    dh2 = g.sum_chips(sum_cols(d_second))
    scaled = dh2 * gain_two
    sums = jnp.stack([jnp.sum(scaled, 1), jnp.sum(scaled * normed_two, 1)])
    sums = (sums + g.swap_row(sums)) / D
    d_middle = cot_half.astype(F32) + rstd_two * (
        scaled - sums[0][:, None] - normed_two * sums[1][:, None]
    )
    grad_second = jnp.sum(dh2 * normed_two, axis=0)
    gm_half = d_middle.astype(BF16)
    gm = jnp.concatenate(g.halves(gm_half, g.swap_core(gm_half), g.half), 0)
    dz = spread(gm, w_out, 1).reshape(own, heads, DV)

    grad_group = jnp.sum(dz * swish * on, axis=0).reshape(heads * DV)
    swish_slope = sig * (1.0 + gate * (1.0 - sig))
    d_gate = (dz * on * gain_heads * swish_slope).astype(BF16).reshape(own, heads * DV)
    d_gate_other = g.swap_row(d_gate)
    d_on = dz * swish * gain_heads
    d_retained = rstd_o * (
        d_on
        - jnp.mean(d_on, axis=2, keepdims=True)
        - on * jnp.mean(d_on * on, axis=2, keepdims=True)
    )
    d_retained = d_retained.astype(BF16).reshape(seqs, LEN, heads, DV)
    d_v = jnp.einsum("shcl,schd->slhd", weights, d_retained, preferred_element_type=F32)
    d_v = d_v.astype(BF16).reshape(own, heads * DV)
    d_v_other = g.swap_row(d_v)
    d_weights = jnp.einsum("schd,slhd->shcl", d_retained, v, preferred_element_type=F32)
    d_scores = (d_weights * mask).astype(BF16)
    d_q = jnp.einsum("shcl,slhd->schd", d_scores, k, preferred_element_type=F32)
    d_k = jnp.einsum("shcl,schd->slhd", d_scores, q, preferred_element_type=F32)
    d_q = d_q.astype(BF16).reshape(own, heads * DK)
    d_k = d_k.astype(BF16).reshape(own, heads * DK)
    d_q_other = g.swap_row(d_q)
    d_k_other = g.swap_row(d_k)

    u_keep, u_send = g.halves(u, u_other, g.half)
    mlp = g.scatter_chips(sum_cols(lambda i: mm((u_keep, u_send)[i], w_down, (1, 0))))
    output = roll(g.to_blocks((g.x_block(middle, g.x) + mlp).astype(BF16)))

    def both(a, b):
        return jnp.concatenate([a, b], 0)

    def grad(left, right):
        return g.reduce_dp(mm(left, right, (0, 0)).astype(BF16))

    grad_down = grad(both(u, u_other), cot)
    grad_act = grad(h2, both(d_act, d_act_other))
    grad_lin = grad(h2, both(d_lin, d_lin_other))
    grad_out = grad(both(z, z_other), gm)
    grad_gate = grad(h1, both(d_gate, d_gate_other))
    grad_value = grad(h1, both(d_v, d_v_other))
    grad_query = grad(h1, both(d_q, d_q_other))
    grad_key = grad(h1, both(d_k, d_k_other))

    pairs = [
        (g.halves(d_gate, d_gate_other, g.half), w_gate),
        (g.halves(d_v, d_v_other, g.half), w_value),
        (g.halves(d_q, d_q_other, g.half), w_query),
        (g.halves(d_k, d_k_other, g.half), w_key),
    ]
    dh1 = g.scatter_chips(
        sum_cols(lambda i: sum(mm(rows[i], weight, (1, 1)) for rows, weight in pairs))
    )
    one_half = g.x_block(g.pick(g.half, normed_one[:own], normed_one[own:]), g.x)
    gain_x = g.x_block(gain_one[None], g.x)
    rstd_half = g.pick(g.half, rstd_one[:own], rstd_one[own:])[:, None]
    scaled = dh1 * gain_x
    sums = jnp.stack([jnp.sum(scaled, 1), jnp.sum(scaled * one_half, 1)])
    for bit in g.x_bits:
        sums = sums + g.swap_col(sums, bit)
    sums = (sums + g.swap_row(sums)) / D
    grad_input = g.x_block(d_middle, g.x) + rstd_half * (
        scaled - sums[0][:, None] - one_half * sums[1][:, None]
    )
    grad_input = roll(g.to_blocks(grad_input))
    grad_first = jnp.sum(dh1 * one_half, axis=0)

    norm_gains = jnp.stack([grad_first, g.x_block(grad_second[None], g.x)[0]])
    norm_gains = norm_gains + g.swap_core(norm_gains)
    width = norm_gains.shape[1] // 2
    norm_gains = g.pick(g.core, norm_gains[:, :width], norm_gains[:, width:])
    grad_group = grad_group + g.swap_row(grad_group)
    small = jnp.concatenate([norm_gains[0], norm_gains[1], grad_group])[None]
    bit = 1
    while bit < g.dp:
        small = small + lax.ppermute(small, "dp", [(i, i ^ bit) for i in range(g.dp)])
        bit *= 2
    small = small[0]
    grad_first, grad_second, grad_group = small[:width], small[width : 2 * width], small[2 * width :]

    return (
        output,
        grad_input,
        grad_query,
        grad_key,
        grad_value,
        grad_gate,
        grad_out,
        grad_act,
        grad_lin,
        grad_down,
        grad_first,
        grad_second,
        grad_group,
    )


def solution(mesh):
    in_specs = (
        P("dp", ("row", "col")),
        P(("dp", "row")),
        P(("row", "col")),
        P("row", "col"),
        P("row", "col"),
        P("row", "col"),
        P("row", "col"),
        P("col"),
        P("col", "row"),
        P(("row", "col")),
        P("row", "col"),
        P("row", "col"),
        P("col", "row"),
        P("dp", ("row", "col")),
    )
    out_specs = (
        P("dp", ("row", "col")),
        P("dp", ("row", "col")),
        P("row", "col"),
        P("row", "col"),
        P("row", "col"),
        P("row", "col"),
        P("col", "row"),
        P("row", "col"),
        P("row", "col"),
        P("col", "row"),
        P(("row", "col")),
        P(("row", "col")),
        P("col"),
    )
    return jax.shard_map(body, mesh=mesh, in_specs=in_specs, out_specs=out_specs, check_vma=False)
```
